32 devices in a mesh: dp: 16 (over z, x, core), tensor: 2 (over y).
Axes of the slice: x: 2, y: 2, z: 4, core: 2. Of those that a mesh axis runs over, the one named last changes fastest.
Arguments:
- tokens: bfloat16 [16, 736, 1152], P('dp', 'tensor'), may hold values from -6 to 6
- cotangent: bfloat16 [16, 736, 1152], P('dp', 'tensor'), may hold values from -6 to 6
- counts: int32 [16], P('dp'), may hold values from 638 to 729
- joint_weight: float32 [1152, 3, 1152], P('dp', None, 'tensor'), may hold values from -0.1875 to 0.1875
- joint_moment: float32 [1152, 3, 1152], P('dp', None, 'tensor'), may hold values from -0.0014648438 to 0.0014648438
- joint_square: float32 [1152, 3, 1152], P('dp', None, 'tensor'), may hold values from 4.53793e-09 to 3.630344e-08
- output_weight: float32 [1152, 1152], P('tensor', 'dp'), may hold values from -0.5 to 0.5
- output_moment: float32 [1152, 1152], P('tensor', 'dp'), may hold values from -0.0029296875 to 0.0029296875
- output_square: float32 [1152, 1152], P('tensor', 'dp'), may hold values from 1.815172e-08 to 1.4521376e-07
- expand_weight: float32 [1152, 4304], P('dp', 'tensor'), may hold values from -0.1875 to 0.1875
- expand_moment: float32 [1152, 4304], P('dp', 'tensor'), may hold values from -0.0029296875 to 0.0029296875
- expand_square: float32 [1152, 4304], P('dp', 'tensor'), may hold values from 1.815172e-08 to 1.4521376e-07
- reduce_weight: float32 [4304, 1152], P('tensor', 'dp'), may hold values from -0.09375 to 0.09375
- reduce_moment: float32 [4304, 1152], P('tensor', 'dp'), may hold values from -0.005859375 to 0.005859375
- reduce_square: float32 [4304, 1152], P('tensor', 'dp'), may hold values from 7.260688e-08 to 5.8085504e-07
- norm_gains: float32 [2, 1152], replicated, may hold values from 0.5 to 1.5
- gains_moment: float32 [2, 1152], replicated, may hold values from -0.009765625 to 0.009765625
- gains_square: float32 [2, 1152], replicated, may hold values from 2.0168576e-07 to 1.6134861e-06
- shifts: float32 [4, 1152], replicated, may hold values from -3 to 3
- shifts_moment: float32 [4, 1152], replicated, may hold values from -0.009765625 to 0.009765625
- shifts_square: float32 [4, 1152], replicated, may hold values from 2.0168576e-07 to 1.6134861e-06
- head_bias: float32 [2, 1152], P(None, 'tensor'), may hold values from -3 to 3
- head_moment: float32 [2, 1152], P(None, 'tensor'), may hold values from -0.0029296875 to 0.0029296875
- head_square: float32 [2, 1152], P(None, 'tensor'), may hold values from 1.815172e-08 to 1.4521376e-07
- hidden_bias: float32 [4304], P('tensor'), may hold values from -3 to 3
- hidden_moment: float32 [4304], P('tensor'), may hold values from -0.0029296875 to 0.0029296875
- hidden_square: float32 [4304], P('tensor'), may hold values from 1.815172e-08 to 1.4521376e-07
Outputs:
- layer_out: bfloat16 [16, 736, 1152], P('dp', 'tensor')
- input_grad: bfloat16 [16, 736, 1152], P('dp', 'tensor')
- grad_norm: float32 [], replicated
- joint_new: float32 [1152, 3, 1152], P('dp', None, 'tensor')
- joint_moment_new: float32 [1152, 3, 1152], P('dp', None, 'tensor')
- joint_square_new: float32 [1152, 3, 1152], P('dp', None, 'tensor')
- joint_copy: bfloat16 [1152, 3, 1152], P('dp', None, 'tensor')
- output_new: float32 [1152, 1152], P('tensor', 'dp')
- output_moment_new: float32 [1152, 1152], P('tensor', 'dp')
- output_square_new: float32 [1152, 1152], P('tensor', 'dp')
- output_copy: bfloat16 [1152, 1152], P('tensor', 'dp')
- expand_new: float32 [1152, 4304], P('dp', 'tensor')
- expand_moment_new: float32 [1152, 4304], P('dp', 'tensor')
- expand_square_new: float32 [1152, 4304], P('dp', 'tensor')
- expand_copy: bfloat16 [1152, 4304], P('dp', 'tensor')
- reduce_new: float32 [4304, 1152], P('tensor', 'dp')
- reduce_moment_new: float32 [4304, 1152], P('tensor', 'dp')
- reduce_square_new: float32 [4304, 1152], P('tensor', 'dp')
- reduce_copy: bfloat16 [4304, 1152], P('tensor', 'dp')
- gains_new: float32 [2, 1152], replicated
- gains_moment_new: float32 [2, 1152], replicated
- gains_square_new: float32 [2, 1152], replicated
- shifts_new: float32 [4, 1152], replicated
- shifts_moment_new: float32 [4, 1152], replicated
- shifts_square_new: float32 [4, 1152], replicated
- head_new: float32 [2, 1152], P(None, 'tensor')
- head_moment_new: float32 [2, 1152], P(None, 'tensor')
- head_square_new: float32 [2, 1152], P(None, 'tensor')
- hidden_new: float32 [4304], P('tensor')
- hidden_moment_new: float32 [4304], P('tensor')
- hidden_square_new: float32 [4304], P('tensor')
The draws below stay inside these ranges and needn't reach their ends.
Inputs may be any that keep to these rules, and one draw needn't show every extreme that they name: `counts`: valid tokens of each image; key slots from there up to 736 are padding.
All inputs are finite; a program needn't handle non-finite values.
Results may differ from the reference program's by a relative error of at most 0.01.
Values may be sent and summed in bfloat16 or wider, within the bound.
A program may use at most 192 MiB of HBM per device.

```python
import math
import jax
import jax.numpy as jnp
from jax import lax

D = 1152
H = 16
HD = 72
FF = 4304
SEQ = 736
VALID = 729
STEP = 4
IMAGES = 16


def plant(array, key, low, largest):
    spot = [jax.random.randint(jax.random.fold_in(key, axis), (), 0, length) for axis, length in enumerate(array.shape)]
    longest = array.shape.index(max(array.shape))
    beside = spot[:longest] + [(spot[longest] + 1) % array.shape[longest]] + spot[longest + 1:]
    return array.at[tuple(spot)].set(low).at[tuple(beside)].set(largest)


def raised(drawn, rng, source, target, shards_of, factor):
    owner, partner = [(jnp.arange(drawn.shape[position]) // (drawn.shape[position] // shards_of)).reshape([-1 if axis == position else 1 for axis in range(drawn.ndim)]) for position in (source, target)]
    chosen = jax.random.permutation(rng, shards_of)[partner]
    strong = (owner == chosen) | (owner == (partner + shards_of // 2) % shards_of)
    return jnp.where(strong, factor * drawn, drawn)


def shard_levels(key, dims, pieces, low, largest):
    loudness, own = 1.0, jax.random.fold_in(key, 6)
    for position, shards_of in pieces:
        steps = jnp.exp(jax.random.uniform(jax.random.fold_in(own, position), (shards_of,), jnp.float32, low / len(pieces), largest / len(pieces)))
        loudness = loudness * jnp.repeat(steps, dims[position] // shards_of).reshape([-1 if axis == position else 1 for axis in range(len(dims))])
    return loudness


def noise(own_key, dims, scale, limit, split=(), kind=jnp.bfloat16):
    values = scale * jax.random.normal(own_key, dims, jnp.float32)
    if split:
        values = values * shard_levels(own_key, dims, split, -0.22, 0.18)
    return jnp.clip(values, -limit, limit).astype(kind)


def heavy_noise(rng, shape, scale, bound, pieces, heavy, kind=jnp.bfloat16):
    values = scale * jax.random.normal(rng, shape, jnp.float32)
    if pieces:
        values = values * shard_levels(rng, shape, pieces, -0.22, 0.18)
    return jnp.clip(raised(values, jax.random.fold_in(rng, 3), *heavy), -bound, bound).astype(kind)


def setup_inputs(seed: int = 0) -> dict:
    seeds = jax.random.split(jax.random.key(seed), 28)
    tokens = heavy_noise(seeds[0], (IMAGES, SEQ, D), 1.0, 6.0, ((0, 16), (1, 2)), (0, 2, 16, 2.0))
    cotangent = heavy_noise(seeds[1], (IMAGES, SEQ, D), 1.0, 6.0, ((0, 16), (1, 2)), (0, 2, 16, 2.0))
    counts = plant(jax.random.randint(seeds[2], (IMAGES,), VALID - VALID // 8, VALID + 1), jax.random.fold_in(seeds[2], 1), VALID - VALID // 8, VALID).astype(jnp.int32)
    joint_weight = noise(seeds[3], (D, 3, H * HD), D ** -0.5, 0.1875, ((0, 16), (2, 2)), jnp.float32)
    joint_moment = noise(seeds[4], (D, 3, H * HD), (0.21 / (D * FF) ** 0.5), 0.0014648438, ((0, 16), (2, 2)), jnp.float32)
    joint_square = jnp.clip(jnp.exp(math.log(3.630344025395971e-08) - 2.0794415 * jax.random.uniform(seeds[5], (D, 3, H * HD), jnp.float32) ** shard_levels(seeds[5], (D, 3, H * HD), ((0, 16), (2, 2)), -0.2, 0.2)), 4.537930031744963e-09, 3.630344025395971e-08)
    output_weight = noise(seeds[6], (H * HD, D), (H * HD // 8) ** -0.5, 0.5, ((0, 2), (1, 16)), jnp.float32)
    output_moment = noise(seeds[7], (H * HD, D), (0.42 / (D * FF) ** 0.5), 0.0029296875, ((0, 2), (1, 16)), jnp.float32)
    output_square = jnp.clip(jnp.exp(math.log(1.4521376101583883e-07) - 2.0794415 * jax.random.uniform(seeds[8], (H * HD, D), jnp.float32) ** shard_levels(seeds[8], (H * HD, D), ((0, 2), (1, 16)), -0.2, 0.2)), 1.8151720126979853e-08, 1.4521376101583883e-07)
    expand_weight = noise(seeds[9], (D, FF), D ** -0.5, 0.1875, ((0, 16), (1, 2)), jnp.float32)
    expand_moment = noise(seeds[10], (D, FF), (0.42 / (D * FF) ** 0.5), 0.0029296875, ((0, 16), (1, 2)), jnp.float32)
    expand_square = jnp.clip(jnp.exp(math.log(1.4521376101583883e-07) - 2.0794415 * jax.random.uniform(seeds[11], (D, FF), jnp.float32) ** shard_levels(seeds[11], (D, FF), ((0, 16), (1, 2)), -0.2, 0.2)), 1.8151720126979853e-08, 1.4521376101583883e-07)
    reduce_weight = noise(seeds[12], (FF, D), FF ** -0.5, 0.09375, ((0, 2), (1, 16)), jnp.float32)
    reduce_moment = noise(seeds[13], (FF, D), (0.85 / (D * FF) ** 0.5), 0.005859375, ((0, 2), (1, 16)), jnp.float32)
    reduce_square = jnp.clip(jnp.exp(math.log(5.808550440633553e-07) - 2.0794415 * jax.random.uniform(seeds[14], (FF, D), jnp.float32) ** shard_levels(seeds[14], (FF, D), ((0, 2), (1, 16)), -0.2, 0.2)), 7.260688050791941e-08, 5.808550440633553e-07)
    norm_gains = jnp.clip(1.0 + 0.1 * jax.random.normal(seeds[15], (2, D), jnp.float32), 0.5, 1.5)
    gains_moment = noise(seeds[16], (2, D), (1.4 / (D * FF) ** 0.5), 0.009765625, (), jnp.float32)
    gains_square = jnp.clip(jnp.exp(jax.random.uniform(seeds[17], (2, D), jnp.float32, math.log(2.0168576497781032e-07), math.log(1.6134861198224826e-06))), 2.0168576497781032e-07, 1.6134861198224826e-06)
    shifts = noise(seeds[18], (4, D), 0.5, 3.0, (), jnp.float32)
    shifts_moment = noise(seeds[19], (4, D), (1.4 / (D * FF) ** 0.5), 0.009765625, (), jnp.float32)
    shifts_square = jnp.clip(jnp.exp(jax.random.uniform(seeds[20], (4, D), jnp.float32, math.log(2.0168576497781032e-07), math.log(1.6134861198224826e-06))), 2.0168576497781032e-07, 1.6134861198224826e-06)
    head_bias = noise(seeds[21], (2, H * HD), 0.5, 3.0, ((1, 2),), jnp.float32)
    head_moment = noise(seeds[22], (2, H * HD), (0.42 / (D * FF) ** 0.5), 0.0029296875, ((1, 2),), jnp.float32)
    head_square = jnp.clip(jnp.exp(math.log(1.4521376101583883e-07) - 2.0794415 * jax.random.uniform(seeds[23], (2, H * HD), jnp.float32) ** shard_levels(seeds[23], (2, H * HD), ((1, 2),), -0.2, 0.2)), 1.8151720126979853e-08, 1.4521376101583883e-07)
    hidden_bias = noise(seeds[24], (FF,), 0.5, 3.0, ((0, 2),), jnp.float32)
    hidden_moment = noise(seeds[25], (FF,), (0.42 / (D * FF) ** 0.5), 0.0029296875, ((0, 2),), jnp.float32)
    hidden_square = jnp.clip(jnp.exp(math.log(1.4521376101583883e-07) - 2.0794415 * jax.random.uniform(seeds[26], (FF,), jnp.float32) ** shard_levels(seeds[26], (FF,), ((0, 2),), -0.2, 0.2)), 1.8151720126979853e-08, 1.4521376101583883e-07)
    return dict(tokens=tokens, cotangent=cotangent, counts=counts, joint_weight=joint_weight, joint_moment=joint_moment, joint_square=joint_square, output_weight=output_weight, output_moment=output_moment, output_square=output_square, expand_weight=expand_weight, expand_moment=expand_moment, expand_square=expand_square, reduce_weight=reduce_weight, reduce_moment=reduce_moment, reduce_square=reduce_square, norm_gains=norm_gains, gains_moment=gains_moment, gains_square=gains_square, shifts=shifts, shifts_moment=shifts_moment, shifts_square=shifts_square, head_bias=head_bias, head_moment=head_moment, head_square=head_square, hidden_bias=hidden_bias, hidden_moment=hidden_moment, hidden_square=hidden_square)


@jax.custom_vjp
def low(v):
    return lax.optimization_barrier(v.astype(jnp.bfloat16)).astype(jnp.float32)

@jax.custom_vjp
def low_back(v):
    return v

def low_keep(v):
    return (low(v), None)

def low_pass(kept, grad):
    return (grad,)

def back_keep(v):
    return (v, None)

def back_low(kept, grad):
    return (low(grad),)
low.defvjp(low_keep, low_pass)
low_back.defvjp(back_keep, back_low)
norm_eps = 1e-06
clip_limit = 1.0
matrix_rate = 0.03
vector_rate = 0.3
decay_rate = 0.1
adam_eps = 1e-08
mask_fill = -1e+30

def layer_norm(values, gain, shift):
    center = lax.optimization_barrier(jnp.mean(values, axis=-1, keepdims=True))
    centred = values - center
    spread = lax.optimization_barrier(jnp.mean(centred * centred, axis=-1, keepdims=True))
    return centred * lax.rsqrt(spread + norm_eps) * gain + shift

def product(form, left, right):
    return jnp.einsum(form, left, right, precision=lax.Precision.HIGHEST)

def one_image(params, image, count):
    joint_w, output_w, expand_w, reduce_w, norm_gains, shifts, head_bias, hidden_bias = params
    length = image.shape[0]
    normed = low(layer_norm(image, norm_gains[0], shifts[0]))
    joint = product('sd,dch->sch', normed, joint_w)
    query = low(low_back(joint[:, 0] + head_bias[0])).reshape(length, H, HD)
    keys = low(low_back(joint[:, 1])).reshape(length, H, HD)
    values = low(low_back(joint[:, 2] + head_bias[1])).reshape(length, H, HD)
    scores = product('qhd,khd->hqk', query, keys) * HD ** (-0.5)
    valid = jnp.arange(length, dtype=jnp.int32) < count
    scores = low_back(jnp.where(valid[None, None, :], scores, mask_fill))
    probs = jax.nn.softmax(scores, axis=-1)
    mixed = product('hqk,khd->qhd', low(probs), values).reshape(length, H * HD)
    mixed = low(low_back(mixed))
    branch = low_back(product('sh,hd->sd', mixed, output_w) + shifts[2])
    middle = image + branch
    second = low(layer_norm(middle, norm_gains[1], shifts[1]))
    before = low_back(product('sd,df->sf', second, expand_w) + hidden_bias)
    active = low(jax.nn.gelu(before, approximate=True))
    result = low_back(product('sf,fd->sd', active, reduce_w) + shifts[3])
    return middle + result

def forward(params, images, counts):
    rounded = (low(params[0]), low(params[1]), low(params[2]), low(params[3])) + tuple(params[4:])
    block = jax.checkpoint(lambda pair: one_image(rounded, pair[0], pair[1]))
    return lax.map(block, (images, counts))

def adamw_step(weight, grad, moment, square, factor, rate, decay):
    clipped = grad * factor
    moment_new = 0.5 * moment + 0.5 * clipped
    square_new = 0.5 * square + 0.5 * clipped * clipped
    correct = 1.0 - 0.5 ** STEP
    update = moment_new / correct / (jnp.sqrt(square_new / correct) + adam_eps)
    return (weight - rate * (update + decay * weight), moment_new, square_new)

def reference(tokens, cotangent, counts, joint_weight, joint_moment, joint_square, output_weight, output_moment, output_square, expand_weight, expand_moment, expand_square, reduce_weight, reduce_moment, reduce_square, norm_gains, gains_moment, gains_square, shifts, shifts_moment, shifts_square, head_bias, head_moment, head_square, hidden_bias, hidden_moment, hidden_square):
    images = tokens.astype(jnp.float32)
    params = (joint_weight, output_weight, expand_weight, reduce_weight, norm_gains, shifts, head_bias, hidden_bias)
    outputs, pullback = jax.vjp(lambda weights, inputs: forward(weights, inputs, counts), params, images)
    grads, image_grad = pullback(cotangent.astype(jnp.float32))
    total = jnp.float32(0.0)
    for grad in grads:
        total = total + jnp.sum(grad * grad)
    grad_norm = jnp.sqrt(total)
    factor = clip_limit / jnp.maximum(grad_norm, clip_limit)
    joint = adamw_step(joint_weight, grads[0], joint_moment, joint_square, factor, matrix_rate, decay_rate)
    output = adamw_step(output_weight, grads[1], output_moment, output_square, factor, matrix_rate, decay_rate)
    expand = adamw_step(expand_weight, grads[2], expand_moment, expand_square, factor, matrix_rate, decay_rate)
    reduce_new = adamw_step(reduce_weight, grads[3], reduce_moment, reduce_square, factor, matrix_rate, decay_rate)
    gains = adamw_step(norm_gains, grads[4], gains_moment, gains_square, factor, vector_rate, 0.0)
    shift = adamw_step(shifts, grads[5], shifts_moment, shifts_square, factor, vector_rate, 0.0)
    head = adamw_step(head_bias, grads[6], head_moment, head_square, factor, vector_rate, 0.0)
    hidden = adamw_step(hidden_bias, grads[7], hidden_moment, hidden_square, factor, vector_rate, 0.0)
    return (outputs.astype(jnp.bfloat16), image_grad.astype(jnp.bfloat16), grad_norm, joint[0], joint[1], joint[2], joint[0].astype(jnp.bfloat16), output[0], output[1], output[2], output[0].astype(jnp.bfloat16), expand[0], expand[1], expand[2], expand[0].astype(jnp.bfloat16), reduce_new[0], reduce_new[1], reduce_new[2], reduce_new[0].astype(jnp.bfloat16), gains[0], gains[1], gains[2], shift[0], shift[1], shift[2], head[0], head[1], head[2], hidden[0], hidden[1], hidden[2])
```

```python
import jax
import jax.numpy as jnp
from jax import lax
from jax.sharding import PartitionSpec as P

HD = 72
STEP = 4


norm_eps = 1e-06
clip_limit = 1.0
matrix_rate = 0.03
vector_rate = 0.3
decay_rate = 0.1
adam_eps = 1e-08
mask_fill = -1e30


def layer_norm(values, gain, shift):
    center = jnp.mean(values, axis=-1, keepdims=True)
    centred = values - center
    spread = jnp.mean(centred * centred, axis=-1, keepdims=True)
    return centred * lax.rsqrt(spread + norm_eps) * gain + shift


def gelu_tanh(values):
    return jax.nn.gelu(values, approximate=True)


def whole_rows(part):
    return lax.all_gather(part, "tensor", axis=1, tiled=True)


def share_rows(full):
    return lax.psum_scatter(
        full.astype(jnp.bfloat16), "tensor", scatter_dimension=1, tiled=True
    ).astype(jnp.float32)


def scatter_sum(part, dim):
    return lax.psum_scatter(
        part.astype(jnp.bfloat16), "dp", scatter_dimension=dim, tiled=True
    ).astype(jnp.float32)


def split_heads(joint):
    length = joint.shape[0]
    heads_local = joint.shape[2] // HD
    query = joint[:, 0].reshape(length, heads_local, HD)
    keys = joint[:, 1].reshape(length, heads_local, HD)
    values = joint[:, 2].reshape(length, heads_local, HD)
    return (query, keys, values)


def masked_scores(query, keys, count):
    length = query.shape[0]
    scores = jnp.einsum("qhd,khd->hqk", query, keys, preferred_element_type=jnp.float32) * HD ** (
        -0.5
    )
    valid = jnp.arange(length, dtype=jnp.int32) < count
    return jnp.where(valid[None, None, :], scores, mask_fill)


def attend(joint, count):
    query, keys, values = split_heads(joint)
    scores = masked_scores(query, keys, count)
    top = jnp.max(scores, axis=-1, keepdims=True)
    total = jnp.sum(jnp.exp(scores - top), axis=-1, keepdims=True)
    logsum = top + jnp.log(total)
    probs = jnp.exp(scores - logsum)
    mixed = jnp.einsum(
        "hqk,khd->qhd", probs.astype(jnp.bfloat16), values, preferred_element_type=jnp.float32
    )
    return (mixed.reshape(joint.shape[0], joint.shape[2]).astype(jnp.bfloat16), logsum[:, :, 0])


def attend_back(joint, mixed_grad, logsum, count):
    query, keys, values = split_heads(joint)
    length = joint.shape[0]
    grad_heads = mixed_grad.reshape(length, joint.shape[2] // HD, HD)
    scores = masked_scores(query, keys, count)
    probs = jnp.exp(scores - logsum[:, :, None])
    value_grad = jnp.einsum(
        "hqk,qhd->khd", probs.astype(jnp.bfloat16), grad_heads, preferred_element_type=jnp.float32
    )
    prob_grad = jnp.einsum("qhd,khd->hqk", grad_heads, values, preferred_element_type=jnp.float32)
    inner = jnp.sum(probs * prob_grad, axis=-1, keepdims=True)
    score_grad = (probs * (prob_grad - inner)).astype(jnp.bfloat16)
    query_grad = jnp.einsum(
        "hqk,khd->qhd", score_grad, keys, preferred_element_type=jnp.float32
    ) * HD ** (-0.5)
    key_grad = jnp.einsum(
        "hqk,qhd->khd", score_grad, query, preferred_element_type=jnp.float32
    ) * HD ** (-0.5)
    stacked = jnp.stack([query_grad, key_grad, value_grad], axis=1)
    return stacked.reshape(length, 3, joint.shape[2]).astype(jnp.bfloat16)


def forward_pass(tokens, counts, weights, small):
    joint_w, expand_w, output_w, reduce_w = weights
    norm_gains, shifts, head_bias, hidden_bias = small
    rows = tokens.astype(jnp.float32)
    normed, first_back = jax.vjp(layer_norm, rows, norm_gains[0], shifts[0])
    normed_whole = whole_rows(normed.astype(jnp.bfloat16))
    joint = jnp.einsum("bsd,dch->bsch", normed_whole, joint_w, preferred_element_type=jnp.float32)
    bias = jnp.stack([head_bias[0], jnp.zeros_like(head_bias[0]), head_bias[1]])
    joint = (joint + bias).astype(jnp.bfloat16)
    mixed, logsum = lax.map(lambda pair: attend(pair[0], pair[1]), (joint, counts))
    branch = (
        share_rows(jnp.einsum("bsh,hd->bsd", mixed, output_w, preferred_element_type=jnp.float32))
        + shifts[2]
    )
    middle = rows + branch
    second, second_back = jax.vjp(layer_norm, middle, norm_gains[1], shifts[1])
    second_whole = whole_rows(second.astype(jnp.bfloat16))
    before = (
        jnp.einsum("bsd,df->bsf", second_whole, expand_w, preferred_element_type=jnp.float32)
        + hidden_bias
    )
    active, gelu_back = jax.vjp(gelu_tanh, before)
    active = active.astype(jnp.bfloat16)
    result = (
        share_rows(jnp.einsum("bsf,fd->bsd", active, reduce_w, preferred_element_type=jnp.float32))
        + shifts[3]
    )
    saved = (
        first_back,
        normed_whole,
        joint,
        mixed,
        logsum,
        second_back,
        second_whole,
        active,
        gelu_back,
    )
    return (middle + result, saved)


def adamw_step(weight, grad, moment, square, factor, rate, decay):
    clipped = grad * factor
    moment_new = 0.5 * moment + 0.5 * clipped
    square_new = 0.5 * square + 0.5 * clipped * clipped
    correct = 1.0 - 0.5**STEP
    update = moment_new / correct / (jnp.sqrt(square_new / correct) + adam_eps)
    return (weight - rate * (update + decay * weight), moment_new, square_new)


def squares(values):
    return jnp.sum(values * values)


def on_device(
    tokens,
    cotangent,
    counts,
    joint_weight,
    joint_moment,
    joint_square,
    output_weight,
    output_moment,
    output_square,
    expand_weight,
    expand_moment,
    expand_square,
    reduce_weight,
    reduce_moment,
    reduce_square,
    norm_gains,
    gains_moment,
    gains_square,
    shifts,
    shifts_moment,
    shifts_square,
    head_bias,
    head_moment,
    head_square,
    hidden_bias,
    hidden_moment,
    hidden_square,
):
    first_pair = (
        lax.all_gather(joint_weight.astype(jnp.bfloat16), "dp", axis=0, tiled=True),
        lax.all_gather(expand_weight.astype(jnp.bfloat16), "dp", axis=0, tiled=True),
    )
    second_pair = (
        lax.all_gather(output_weight.astype(jnp.bfloat16), "dp", axis=1, tiled=True),
        lax.all_gather(reduce_weight.astype(jnp.bfloat16), "dp", axis=1, tiled=True),
    )
    weights = (first_pair[0], first_pair[1], second_pair[0], second_pair[1])
    small = (norm_gains, shifts, head_bias, hidden_bias)
    layer_rows, saved = forward_pass(tokens, counts, weights, small)
    layer_out = layer_rows.astype(jnp.bfloat16)
    first_back, normed_whole, joint, mixed, logsum, second_back, second_whole, active, gelu_back = (
        saved
    )
    joint_w, expand_w, output_w, reduce_w = weights
    grad_rows = cotangent.astype(jnp.float32)
    grad_whole = whole_rows(cotangent)
    reduce_grad = jnp.einsum("bsf,bsd->fd", active, grad_whole, preferred_element_type=jnp.float32)
    active_grad = jnp.einsum(
        "bsd,fd->bsf", grad_whole, reduce_w, preferred_element_type=jnp.float32
    )
    before_grad = gelu_back(active_grad)[0].astype(jnp.bfloat16)
    expand_grad = jnp.einsum(
        "bsd,bsf->df", second_whole, before_grad, preferred_element_type=jnp.float32
    )
    hidden_grad = jnp.sum(before_grad, axis=(0, 1), dtype=jnp.float32)
    second_grad = share_rows(
        jnp.einsum("bsf,df->bsd", before_grad, expand_w, preferred_element_type=jnp.float32)
    )
    middle_part, gain_two, shift_two = second_back(second_grad)
    middle_grad = grad_rows + middle_part
    branch_grad = middle_grad.astype(jnp.bfloat16)
    branch_whole = whole_rows(branch_grad)
    output_grad = jnp.einsum("bsh,bsd->hd", mixed, branch_whole, preferred_element_type=jnp.float32)
    mixed_grad = jnp.einsum(
        "bsd,hd->bsh", branch_whole, output_w, preferred_element_type=jnp.float32
    ).astype(jnp.bfloat16)
    joint_grad = lax.map(
        lambda group: attend_back(group[0], group[1], group[2], group[3]),
        (joint, mixed_grad, logsum, counts),
    )
    joint_weight_grad = jnp.einsum(
        "bsd,bsch->dch", normed_whole, joint_grad, preferred_element_type=jnp.float32
    )
    head_grad = jnp.sum(joint_grad[:, :, 0::2], axis=(0, 1), dtype=jnp.float32)
    first_grad = share_rows(
        jnp.einsum("bsch,dch->bsd", joint_grad, joint_w, preferred_element_type=jnp.float32)
    )
    rows_part, gain_one, shift_one = first_back(first_grad)
    input_grad = (middle_grad + rows_part).astype(jnp.bfloat16)
    gain_grad = jnp.stack([gain_one, gain_two])
    shift_grad = jnp.stack(
        [
            shift_one,
            shift_two,
            jnp.sum(branch_grad, axis=(0, 1), dtype=jnp.float32),
            jnp.sum(grad_rows, axis=(0, 1)),
        ]
    )
    joint_sum, expand_sum = (
        scatter_sum(joint_weight_grad, 0),
        scatter_sum(expand_grad, 0),
    )
    output_sum, reduce_sum = (
        scatter_sum(output_grad, 1),
        scatter_sum(reduce_grad, 1),
    )
    gain_sum, shift_sum = lax.psum((gain_grad, shift_grad), ("dp", "tensor"))
    head_sum, hidden_sum = lax.psum((head_grad, hidden_grad), "dp")
    data_count = lax.axis_size("dp")
    split_count = lax.axis_size("tensor")
    owned = squares(joint_sum) + squares(expand_sum) + squares(output_sum) + squares(reduce_sum)
    shared = (squares(head_sum) + squares(hidden_sum)) / data_count
    everywhere = (squares(gain_sum) + squares(shift_sum)) / (data_count * split_count)
    grad_norm = jnp.sqrt(lax.psum(owned + shared + everywhere, ("dp", "tensor")))
    factor = clip_limit / jnp.maximum(grad_norm, clip_limit)
    joint_state = adamw_step(
        joint_weight, joint_sum, joint_moment, joint_square, factor, matrix_rate, decay_rate
    )
    output_state = adamw_step(
        output_weight, output_sum, output_moment, output_square, factor, matrix_rate, decay_rate
    )
    expand_state = adamw_step(
        expand_weight, expand_sum, expand_moment, expand_square, factor, matrix_rate, decay_rate
    )
    reduce_state = adamw_step(
        reduce_weight, reduce_sum, reduce_moment, reduce_square, factor, matrix_rate, decay_rate
    )
    gains_state = adamw_step(
        norm_gains, gain_sum, gains_moment, gains_square, factor, vector_rate, 0.0
    )
    shifts_state = adamw_step(
        shifts, shift_sum, shifts_moment, shifts_square, factor, vector_rate, 0.0
    )
    head_state = adamw_step(head_bias, head_sum, head_moment, head_square, factor, vector_rate, 0.0)
    hidden_state = adamw_step(
        hidden_bias, hidden_sum, hidden_moment, hidden_square, factor, vector_rate, 0.0
    )
    return (
        layer_out,
        input_grad,
        grad_norm,
        joint_state[0],
        joint_state[1],
        joint_state[2],
        joint_state[0].astype(jnp.bfloat16),
        output_state[0],
        output_state[1],
        output_state[2],
        output_state[0].astype(jnp.bfloat16),
        expand_state[0],
        expand_state[1],
        expand_state[2],
        expand_state[0].astype(jnp.bfloat16),
        reduce_state[0],
        reduce_state[1],
        reduce_state[2],
        reduce_state[0].astype(jnp.bfloat16),
        gains_state[0],
        gains_state[1],
        gains_state[2],
        shifts_state[0],
        shifts_state[1],
        shifts_state[2],
        head_state[0],
        head_state[1],
        head_state[2],
        hidden_state[0],
        hidden_state[1],
        hidden_state[2],
    )


def solution(mesh):
    in_specs = (
        P("dp", "tensor", None),
        P("dp", "tensor", None),
        P("dp"),
        P("dp", None, "tensor"),
        P("dp", None, "tensor"),
        P("dp", None, "tensor"),
        P("tensor", "dp"),
        P("tensor", "dp"),
        P("tensor", "dp"),
        P("dp", "tensor"),
        P("dp", "tensor"),
        P("dp", "tensor"),
        P("tensor", "dp"),
        P("tensor", "dp"),
        P("tensor", "dp"),
        P(),
        P(),
        P(),
        P(),
        P(),
        P(),
        P(None, "tensor"),
        P(None, "tensor"),
        P(None, "tensor"),
        P("tensor"),
        P("tensor"),
        P("tensor"),
    )
    out_specs = (
        P("dp", "tensor", None),
        P("dp", "tensor", None),
        P(),
        P("dp", None, "tensor"),
        P("dp", None, "tensor"),
        P("dp", None, "tensor"),
        P("dp", None, "tensor"),
        P("tensor", "dp"),
        P("tensor", "dp"),
        P("tensor", "dp"),
        P("tensor", "dp"),
        P("dp", "tensor"),
        P("dp", "tensor"),
        P("dp", "tensor"),
        P("dp", "tensor"),
        P("tensor", "dp"),
        P("tensor", "dp"),
        P("tensor", "dp"),
        P("tensor", "dp"),
        P(),
        P(),
        P(),
        P(),
        P(),
        P(),
        P(None, "tensor"),
        P(None, "tensor"),
        P(None, "tensor"),
        P("tensor"),
        P("tensor"),
        P("tensor"),
    )
    return jax.shard_map(
        on_device, mesh=mesh, in_specs=in_specs, out_specs=out_specs, check_vma=False
    )
```
